256 devices in a mesh: dp: 2 (over y_hi), pipe: 16 (over y_lo, x, core), seq: 8 (over z).
Axes of the slice: x: 4, y: 4 (y_hi: 2, y_lo: 2; y = y_hi * 2 + y_lo), z: 8, core: 2. Of those that a mesh axis runs over, the one named last changes fastest.
Arguments:
- enc_out: bfloat16 [2, 512, 4096], P('dp', None, 'seq'), may hold values from -60 to 60
- w_key: bfloat16 [16, 4096, 2048], P('pipe', None, 'seq'), may hold values from -0.125 to 0.125
- w_value: bfloat16 [16, 4096, 2048], P('pipe', None, 'seq'), may hold values from -0.125 to 0.125
- query: bfloat16 [16, 2, 512, 2048], P('pipe', 'dp', None, 'seq'), may hold values from -256 to 256
- key_cache: bfloat16 [16, 2, 512, 2048], P('pipe', 'dp', None, 'seq'), may hold values from -6 to 6
- value_cache: bfloat16 [16, 2, 512, 2048], P('pipe', 'dp', None, 'seq'), may hold values from -6 to 6
- grad_attn: bfloat16 [16, 2, 512, 2048], P('pipe', 'dp', None, 'seq'), may hold values from -200 to 200
- dec_segments: int32 [2, 512], P('dp'), may hold values from 0 to 3, as said below
- enc_segments: int32 [2, 512], P('dp'), may hold values from 0 to 3, as said below
Outputs:
- grad_query: bfloat16 [16, 2, 512, 2048], P('pipe', 'dp', None, 'seq')
- grad_enc: float32 [2, 512, 4096], P('dp', 'seq', 'pipe')
- grad_wkey: float32 [16, 4096, 2048], P('pipe', 'dp', 'seq')
- grad_wvalue: float32 [16, 4096, 2048], P('pipe', 'dp', 'seq')
The draws below stay inside these ranges and needn't reach their ends.
Inputs may be any that keep to these rules, and one draw needn't show every extreme that they name: `dec_segments`: never falling along a sequence; every number from 0 to 3 occurs; a segment holds 1 to 256 tokens, and one holds exactly 256. `enc_segments`: never falling along a sequence; every number from 0 to 3 occurs; a segment holds 1 to 256 tokens, and one holds exactly 256.
All inputs are finite; a program needn't handle non-finite values.
Results may differ from the reference program's by a relative error of at most 0.006.
Values may be sent and summed in bfloat16 or wider, within the bound.
No kernel may reach another device: no remote copies, remote signals or barrier semaphores. Data moves between devices by JAX's collectives and lax.ppermute only.
A program may use at most 128 MiB of HBM per device.

```python
import math
import jax
import jax.numpy as jnp
from jax import lax

D = 4096
H = 8
HD = 256
L = 512
HH = 2048
B = 2
SECTIONS = 16
SEGS = 4
SEG_MOST = 256


def segment_table(key, salt):
    base_key = jax.random.fold_in(key, salt)

    def one_row(row_key):
        key_weights, key_place = jax.random.split(row_key)
        weights = jax.random.randint(key_weights, (SEGS - 1,), 1, 4).astype(jnp.int32)
        running = jnp.cumsum(weights).astype(jnp.int32)
        remaining = L - SEG_MOST
        cut_points = remaining * running // running[-1]
        others = jnp.diff(jnp.concatenate([jnp.zeros((1,), jnp.int32), cut_points]))
        padded = jnp.concatenate([others, jnp.zeros((1,), jnp.int32)])
        slot_place = jax.random.randint(key_place, (), 0, SEGS)
        series = jnp.arange(SEGS)
        before = padded[series]
        after_place = padded[series - 1]
        lengths = jnp.where(series < slot_place, before, jnp.where(series == slot_place, SEG_MOST, after_place))
        seg_ends = jnp.cumsum(lengths)
        positions = jnp.arange(L)
        return jnp.sum(positions[:, None] >= seg_ends[None, :], axis=1).astype(jnp.int32)
    return jax.vmap(one_row)(jax.random.split(base_key, B))


def key_table(key):
    noise = jax.random.normal(jax.random.fold_in(key, 21), (SECTIONS, B, L, HH), jnp.float32)
    return jnp.clip(noise, -6.0, 6.0).astype(jnp.bfloat16)


def draw_dec_segments(key, part):
    return segment_table(key, 11)


def draw_enc_segments(key, part):
    return segment_table(key, 12)


def draw_key_cache(key, part):
    return key_table(key)


def draw_query(key, part):
    key_base = jax.random.fold_in(key, 31)
    shape_all = (SECTIONS, B, L, HH)
    noise = jax.random.normal(key_base, shape_all, jnp.float32)
    return jnp.clip(noise, -6.0, 6.0).astype(jnp.bfloat16)


def draw_grad_attn(key, part):
    shape_all = (SECTIONS, B, L, HH)
    key_base, key_columns = jax.random.split(jax.random.fold_in(key, 41), 2)
    head_of = (jnp.arange(HH) // HD).astype(jnp.float32)
    rising = jnp.exp(math.log(3.0) * head_of / (H - 1))
    column_scale = jnp.exp(jax.random.uniform(key_columns, (HH,), jnp.float32, 0.0, math.log(10.0)))
    base = jnp.clip(jax.random.normal(key_base, shape_all, jnp.float32), -6.0, 6.0)
    result = base * rising * column_scale
    return result.astype(jnp.bfloat16)


def draw_enc_out(key, part):
    key_base, key_scale = jax.random.split(jax.random.fold_in(key, 51), 2)
    feature_scale = jnp.exp(jax.random.uniform(key_scale, (D,), jnp.float32, 0.0, math.log(10.0)))
    base = jnp.clip(jax.random.normal(key_base, (B, L, D), jnp.float32), -6.0, 6.0)
    result = base * feature_scale
    return result.astype(jnp.bfloat16)


def spiked(values, key, source, target, parts, factor):
    def block_of(dim):
        return (jnp.arange(values.shape[dim]) // (values.shape[dim] // parts)).reshape((-1,) + (1,) * (values.ndim - 1 - dim))

    one_side = jax.random.permutation(key, parts)[block_of(target)]
    far = (block_of(target) + parts // 2) % parts
    return jnp.where((block_of(source) == one_side) | (block_of(source) == far), factor * values, values)


def steps_of(own_key, extent, cuts, smallest, largest):
    gain = 1.0
    for axis_at, shards_of in cuts:
        draws = jax.random.uniform(jax.random.fold_in(jax.random.fold_in(own_key, 6), axis_at), (shards_of,), jnp.float32, smallest / len(cuts), largest / len(cuts))
        gain = gain * jnp.repeat(jnp.exp(draws), extent[axis_at] // shards_of).reshape((-1,) + (1,) * (len(extent) - 1 - axis_at))
    return gain


def bell_draw(rng, extent, width, most, shards=(), held_as=jnp.bfloat16):
    gain = steps_of(rng, extent, shards, -0.22, 0.18) if shards else 1.0
    values = jax.random.normal(rng, extent, jnp.float32) * width * gain
    return jnp.minimum(jnp.maximum(values, -most), most).astype(held_as)


def bell_draw_with(stream_key, extent, width, bound, pieces, heavy, held_as=jnp.bfloat16):
    drawn = width * jax.random.normal(stream_key, extent, jnp.float32)
    if pieces:
        drawn = drawn * steps_of(stream_key, extent, pieces, -0.22, 0.18)
    return jnp.clip(spiked(drawn, jax.random.fold_in(stream_key, 3), *heavy), -bound, bound).astype(held_as)


def setup_inputs(seed: int = 0) -> dict:
    streams_of = jax.random.split(jax.random.key(seed), 10)
    return {
        "enc_out": draw_enc_out(jax.random.fold_in(streams_of[9], 71), 0),
        "w_key": bell_draw_with(streams_of[1], (SECTIONS, D, HH), D ** -0.5, 0.125, ((0, 16), (2, 8)), (0, 1, 16, 2.0)),
        "w_value": bell_draw_with(streams_of[2], (SECTIONS, D, HH), D ** -0.5, 0.125, ((0, 16), (2, 8)), (0, 1, 16, 2.0)),
        "query": draw_query(jax.random.fold_in(streams_of[9], 71), 0),
        "key_cache": draw_key_cache(jax.random.fold_in(streams_of[9], 71), 0),
        "value_cache": bell_draw(streams_of[5], (SECTIONS, B, L, HH), 1.0, 6.0, ((0, 16), (1, 2), (3, 8))),
        "grad_attn": draw_grad_attn(jax.random.fold_in(streams_of[9], 71), 0),
        "dec_segments": draw_dec_segments(jax.random.fold_in(streams_of[9], 71), 0),
        "enc_segments": draw_enc_segments(jax.random.fold_in(streams_of[9], 71), 0),
    }


def head_backward(query_heads, key_heads, value_heads, grad_heads, dec_ids, enc_ids):
    length = query_heads.shape[0]
    block_rows = 512 if length % 512 == 0 else length
    block_count = length // block_rows
    inverse_root = 1.0 / math.sqrt(query_heads.shape[2])
    keys_wide = key_heads.astype(jnp.float32)
    values_wide = value_heads.astype(jnp.float32)

    def block_step(partial_value, block_index):
        acc_key, acc_value = partial_value
        offset = block_index * block_rows
        query_block = lax.dynamic_slice_in_dim(query_heads, offset, block_rows, 0).astype(jnp.float32)
        grad_block = lax.dynamic_slice_in_dim(grad_heads, offset, block_rows, 0).astype(jnp.float32)
        ids_block = lax.dynamic_slice_in_dim(dec_ids, offset, block_rows, 0)
        same_segment = ids_block[:, None] == enc_ids[None, :]
        scores = jnp.einsum('qhd,khd->hqk', query_block, keys_wide) * inverse_root
        scores = jnp.where(same_segment[None], scores, -jnp.inf)
        row_max = lax.optimization_barrier(jnp.max(scores, axis=2, keepdims=True))
        exp_scores = jnp.exp(scores - row_max)
        probs_full = exp_scores / lax.optimization_barrier(jnp.sum(exp_scores, axis=2, keepdims=True))
        dprobs = jnp.einsum('qhd,khd->hqk', grad_block, values_wide)
        row_delta = lax.optimization_barrier(jnp.sum(probs_full * dprobs, axis=2, keepdims=True))
        dscores = lax.optimization_barrier((probs_full * (dprobs - row_delta) * inverse_root).astype(jnp.bfloat16)).astype(jnp.float32)
        probs_low = lax.optimization_barrier(probs_full.astype(jnp.bfloat16)).astype(jnp.float32)
        query_grad = jnp.einsum('hqk,khd->qhd', dscores, keys_wide).astype(jnp.bfloat16)
        acc_key = acc_key + jnp.einsum('hqk,qhd->khd', dscores, query_block)
        acc_value = acc_value + jnp.einsum('hqk,qhd->khd', probs_low, grad_block)
        return ((acc_key, acc_value), query_grad)
    zeros_init = jnp.zeros(key_heads.shape, jnp.float32)
    (acc_key, acc_value), query_blocks = lax.scan(block_step, (zeros_init, zeros_init), jnp.arange(block_count, dtype=jnp.int32))
    query_grad = query_blocks.reshape(query_heads.shape)
    return (query_grad, acc_key.astype(jnp.bfloat16), acc_value.astype(jnp.bfloat16))

def reference(enc_out, w_key, w_value, query, key_cache, value_cache, grad_attn, dec_segments, enc_segments):
    head_shape = (L, H, HD)

    def section_step(enc_total, inputs):
        section_wkey, section_wvalue, section_query, section_keys, section_values, section_grad = inputs
        sum_key = jnp.zeros((D, HH), jnp.float32)
        sum_value = jnp.zeros((D, HH), jnp.float32)
        query_grads = []
        for batch_row in range(B):
            query_grad, grad_keys, grad_values = head_backward(section_query[batch_row].reshape(head_shape), section_keys[batch_row].reshape(head_shape), section_values[batch_row].reshape(head_shape), section_grad[batch_row].reshape(head_shape), dec_segments[batch_row], enc_segments[batch_row])
            grad_keys = grad_keys.reshape(L, HH)
            grad_values = grad_values.reshape(L, HH)
            enc_term = jnp.dot(grad_keys, section_wkey.T, preferred_element_type=jnp.float32) + jnp.dot(grad_values, section_wvalue.T, preferred_element_type=jnp.float32)
            enc_total = enc_total.at[batch_row].add(enc_term)
            sum_key = sum_key + jnp.dot(enc_out[batch_row].T, grad_keys, preferred_element_type=jnp.float32)
            sum_value = sum_value + jnp.dot(enc_out[batch_row].T, grad_values, preferred_element_type=jnp.float32)
            query_grads.append(query_grad.reshape(L, HH))
        norm_key = sum_key / jnp.sqrt(jnp.mean(sum_key * sum_key) + 1e-06)
        norm_value = sum_value / jnp.sqrt(jnp.mean(sum_value * sum_value) + 1e-06)
        return (enc_total, (jnp.stack(query_grads), norm_key, norm_value))
    enc_total, (grad_query, grad_wkey, grad_wvalue) = lax.scan(section_step, jnp.zeros((B, L, D), jnp.float32), (w_key, w_value, query, key_cache, value_cache, grad_attn))
    return (grad_query, enc_total, grad_wkey, grad_wvalue)
```

```python
import functools
import math

import jax
import jax.numpy as jnp
from jax import lax
from jax.experimental import pallas as pl
from jax.experimental.pallas import tpu as pltpu
from jax.sharding import PartitionSpec as P

D = 4096
H = 8
HD = 256


F32 = jnp.float32
BF16 = jnp.bfloat16
LAST = (((1,), (1,)), ((), ()))
FIRST = (((0,), (0,)), ((), ()))
PLAIN = (((1,), (0,)), ((), ()))


def dot(a, b, dims):
    return lax.dot_general(a, b, dims, preferred_element_type=F32)


def vmem(n):
    return [pl.BlockSpec(memory_space=pltpu.VMEM)] * n


def call(kernel, out, ins, scratch=(), limit=48 << 20, **cost):
    return pl.pallas_call(
        kernel,
        out_shape=out,
        in_specs=vmem(len(ins)),
        out_specs=jax.tree.map(lambda _: pl.BlockSpec(memory_space=pltpu.VMEM), out),
        scratch_shapes=list(scratch),
        compiler_params=pltpu.CompilerParams(vmem_limit_bytes=limit),
        cost_estimate=pl.CostEstimate(
            flops=cost.get("flops", 0), bytes_accessed=cost.get("size", 0), transcendentals=0
        ),
    )(*ins)


def place():
    at = lax.axis_index("pipe")
    core = lax.rem(at, 2)
    x = lax.rem(lax.div(at, 2), 4)
    low = lax.div(at, 8)
    return low, x, core


def half_kernel(enc_ref, out_ref):
    _, _, core = place()
    start = pl.multiple_of(core * 256, 256)
    block = enc_ref[0, :, pl.ds(start, 256)].astype(F32)
    out_ref[...] = block.T.astype(BF16)


def attention_kernel(dec_ref, enc_ref, q_ref, k_ref, v_ref, g_ref, gq_ref, both_ref):
    inverse_root = 1.0 / math.sqrt(HD)
    q = q_ref[0, 0]
    k = k_ref[0, 0]
    v = v_ref[0, 0]
    g = g_ref[0, 0]
    length = q.shape[0]
    dec = dec_ref[...].astype(F32)
    enc = jnp.broadcast_to(enc_ref[...].astype(F32), (128, length)).T[:, :1]
    scores = dot(k, q, LAST) * inverse_root
    scores = jnp.where(enc == dec, scores, -jnp.inf)
    exps = jnp.exp(scores - jnp.max(scores, axis=0, keepdims=True))
    probs = exps / jnp.sum(exps, axis=0, keepdims=True)
    dprobs = dot(v, g, LAST)
    delta = jnp.sum(probs * dprobs, axis=0, keepdims=True)
    dscores = (probs * (dprobs - delta) * inverse_root).astype(BF16)
    both_ref[:, :HD] = dot(dscores, q, PLAIN).astype(BF16)
    both_ref[:, HD:] = dot(probs.astype(BF16), g, PLAIN).astype(BF16)
    gq_ref[0, 0] = dot(dscores, k, FIRST).astype(BF16)


def weight_rows(m, n, bit):
    low, x, _ = place()
    block = (jnp.bitwise_xor(low, n) * 4 + jnp.bitwise_xor(x, m)) * 2 + bit
    return pl.ds(pl.multiple_of(block * 256, 256), 256)


def term(both_ref, wk_ref, wv_ref, rows):
    return dot(both_ref[:, :HD], wk_ref[0, rows, :], LAST) + dot(
        both_ref[:, HD:], wv_ref[0, rows, :], LAST
    )


def other_core_kernel(both_ref, wk_ref, wv_ref, out_ref):
    _, _, core = place()
    for m in range(4):
        for n in range(2):
            rows = weight_rows(m, n, 1 - core)
            out_ref[m, n] = term(both_ref, wk_ref, wv_ref, rows).astype(BF16)


def own_core_kernel(both_ref, wk_ref, wv_ref, got_ref, sa_ref, ka_ref, sb_ref, kb_ref):
    _, _, core = place()
    half = both_ref.shape[0] // 2
    for m in range(4):
        for n in range(2):
            rows = weight_rows(m, n, core)
            total = term(both_ref, wk_ref, wv_ref, rows) + got_ref[m, n].astype(F32)
            a, b = total[:half], total[half:]
            if m == 0:
                ka_ref[0, n] = a
                kb_ref[0, n] = b
            elif m == 1:
                sa_ref[0, n] = a.astype(BF16)
                kb_ref[1, n] = b
            elif m == 2:
                sa_ref[1, n] = a.astype(BF16)
                sb_ref[1, n] = b.astype(BF16)
            else:
                ka_ref[1, n] = a
                sb_ref[0, n] = b.astype(BF16)


def sums_kernel(*refs):
    steps = (0, -1, 1, -2, 2, -3, 3, 4, 4)
    count = len(steps)
    own, other = refs[:count], refs[count : 2 * count]
    here_ref, there_ref, key_ref, value_ref, square_ref, grads, total = refs[2 * count :]
    grads[0] = here_ref[...]
    grads[1] = there_ref[...]
    total[...] = jnp.zeros_like(total)
    d = lax.axis_index("dp")
    z = lax.axis_index("seq")
    _, _, core = place()
    for i, step in enumerate(steps):
        u = lax.rem(z + step - 4 * d + 16, 8)
        which = lax.div(u, 4)
        chunk = jnp.where(u < 4, u, 7 - u)
        grad = grads[which]
        for refs_of, bit in ((own, core), (other, 1 - core)):
            piece = refs_of[i][...]
            start = chunk * 512 + bit * 256
            if i == count - 1:
                start = start + 128
            rows = pl.ds(pl.multiple_of(start, 128), piece.shape[0])
            total[rows, :] += dot(piece, grad, PLAIN)
    key = total[:, :HD]
    value = total[:, HD:]
    key_ref[...] = key
    value_ref[...] = value
    square_ref[0] = jnp.sum((key * key).reshape(-1, 8, 2, 128), axis=(0, 2))
    square_ref[1] = jnp.sum((value * value).reshape(-1, 8, 2, 128), axis=(0, 2))


def shards(
    enc_out, w_key, w_value, query, key_cache, value_cache, grad_attn, dec_segments, enc_segments
):
    length = query.shape[2]
    columns = query.shape[3]
    shape = jax.ShapeDtypeStruct

    def shift(value, by):
        return lax.ppermute(value, "seq", [(i, (i + by) % 8) for i in range(8)])

    def swap(value, low, x, core):
        mask = low * 8 + x * 2 + core
        return lax.ppermute(value, "pipe", [(i, i ^ mask) for i in range(16)])

    piece = call(half_kernel, shape((256, length), BF16), (enc_out,), size=1 << 20)
    pairs = []
    for b in range(2):
        for z in range(8):
            inside = z // 4 == b
            to = b * 8 + z if inside else (1 - b) * 8 + 7 - z
            pairs.append((b * 8 + z, to))
    held = lax.ppermute(piece, ("dp", "seq"), pairs)

    grad_query, both = call(
        attention_kernel,
        (shape((1, 1, length, columns), BF16), shape((length, 2 * columns), BF16)),
        (dec_segments, enc_segments, query, key_cache, value_cache, grad_attn),
        flops=5 * 2 * 512 * 512 * 256,
        size=2 << 20,
    )
    there = lax.ppermute(both, "dp", [(0, 1), (1, 0)])

    ahead = [held]
    behind = [held]
    for _ in range(3):
        ahead.append(shift(ahead[-1], 1))
        behind.append(shift(behind[-1], -1))
    far = (shift(ahead[3][:128], 1), shift(behind[3][128:], -1))
    own = [held]
    for k in range(1, 4):
        own += [ahead[k], behind[k]]
    own += far
    other = [swap(value, 0, 0, 1) for value in own]

    blocks = shape((4, 2, length, 256), BF16)
    sent = call(
        other_core_kernel, blocks, (both, w_key, w_value), flops=1 << 30, size=5 << 20
    )
    got = swap(sent, 0, 0, 1)
    part = (2, 2, length // 2, 256)
    sa, ka, sb, kb = call(
        own_core_kernel,
        (shape(part, BF16), shape(part, F32), shape(part, BF16), shape(part, F32)),
        (both, w_key, w_value, got),
        flops=1 << 30,
        size=8 << 20,
    )
    ra = swap(sa, 0, 1, 0).astype(F32)
    rb = swap(sb, 0, 3, 0).astype(F32)
    ra2 = swap((ka[1] + ra[1]).astype(BF16), 0, 3, 0).astype(F32)
    rb2 = swap((kb[1] + rb[1]).astype(BF16), 0, 1, 0).astype(F32)
    whole = jnp.concatenate([ka[0] + ra[0] + ra2, kb[0] + rb[0] + rb2], axis=1)
    by_section = whole[0] + swap(whole[1].astype(BF16), 1, 0, 0).astype(F32)
    split = by_section.astype(BF16).reshape(8, length // 8, 256)
    by_head = jnp.sum(lax.all_to_all(split, "seq", 0, 0).astype(F32), axis=0)
    grad_enc = by_head[None]

    pieces = tuple(own) + tuple(other) + (both, there)
    sum_key, sum_value, squares = call(
        sums_kernel,
        (shape((2048, HD), F32), shape((2048, HD), F32), shape((2, 8, 128), F32)),
        pieces,
        scratch=(pltpu.VMEM((2, length, 2 * HD), BF16), pltpu.VMEM((2048, 2 * HD), F32)),
        flops=2 << 30,
        size=10 << 20,
    )
    local = jnp.sum(squares, axis=1)
    spread = jnp.broadcast_to(local[None], (16, 2, 128))
    total = jnp.sum(lax.all_to_all(spread, ("dp", "seq"), 0, 0), axis=(0, 2))
    entries = D * H * HD
    grad_wkey = (sum_key / jnp.sqrt(total[0] / entries + 1e-06))[None]
    grad_wvalue = (sum_value / jnp.sqrt(total[1] / entries + 1e-06))[None]
    return (grad_query, grad_enc, grad_wkey, grad_wvalue)


def solution(mesh):
    in_specs = (
        P("dp", None, "seq"),
        P("pipe", None, "seq"),
        P("pipe", None, "seq"),
        P("pipe", "dp", None, "seq"),
        P("pipe", "dp", None, "seq"),
        P("pipe", "dp", None, "seq"),
        P("pipe", "dp", None, "seq"),
        P("dp", None),
        P("dp", None),
    )
    out_specs = (
        P("pipe", "dp", None, "seq"),
        P("dp", "seq", "pipe"),
        P("pipe", "dp", "seq"),
        P("pipe", "dp", "seq"),
    )
    return jax.shard_map(shards, mesh=mesh, in_specs=in_specs, out_specs=out_specs, check_vma=False)
```

```python
import math

import jax
import jax.numpy as jnp
from jax import lax
from jax.experimental import pallas as pl
from jax.experimental.pallas import tpu as pltpu
from jax.sharding import PartitionSpec as P


D = 4096
H = 8
HD = 256


F32 = jnp.float32
BF16 = jnp.bfloat16
LAST = (((1,), (1,)), ((), ()))
FIRST = (((0,), (0,)), ((), ()))
PLAIN = (((1,), (0,)), ((), ()))
VM = pltpu.VMEM
HB = pltpu.HBM
DMA = pltpu.SemaphoreType.DMA
MIB = 1 << 20
FULL = 63
ATTN = 54
X1, X3, Y1 = (0, 1), (0, 3), (1, 0)
ORDERS = ((X1, X3, Y1), (X3, X1, Y1))
RANGES = (256, 256)
NEAR = (0, -1, 1, -2, 2)
FAR = (-3, 3, 4, 4)


def dot(a, b, dims):
    return lax.dot_general(a, b, dims, preferred_element_type=F32)


def call(kernel, out, ins, spaces, outs=None, scratch=(), limit=12, flops=0, size=0, alias=None):
    outs = outs or (VM,) * len(out)
    return pl.pallas_call(
        kernel,
        out_shape=out,
        in_specs=[pl.BlockSpec(memory_space=m) for m in spaces],
        out_specs=tuple(pl.BlockSpec(memory_space=m) for m in outs),
        scratch_shapes=list(scratch),
        input_output_aliases=alias or {},
        compiler_params=pltpu.CompilerParams(vmem_limit_bytes=limit * MIB),
        cost_estimate=pl.CostEstimate(flops=flops, bytes_accessed=size, transcendentals=0),
    )(*ins)


def place():
    at = lax.axis_index("pipe")
    core = lax.rem(at, 2)
    x = lax.rem(lax.div(at, 2), 4)
    low = lax.div(at, 8)
    return low, x, core


def half_kernel(enc_ref, out_ref, block, sem):
    _, _, core = place()
    start = pl.multiple_of(core * 256, 256)
    copy = pltpu.make_async_copy(enc_ref.at[0, :, pl.ds(start, 256)], block, sem)
    copy.start()
    copy.wait()
    out_ref[...] = block[...].astype(F32).T.astype(BF16)


def attention_kernel(
    dec_hbm, enc_hbm, q_hbm, k_hbm, v_hbm, g_hbm, gq_ref, both_ref, dec, enc, qs, ks, vs, gs, sems
):
    inverse_root = 1.0 / math.sqrt(HD)
    copies = [
        pltpu.make_async_copy(src, dst, sems.at[i])
        for i, (src, dst) in enumerate(
            (
                (k_hbm.at[0, 0], ks),
                (q_hbm.at[0, 0], qs),
                (dec_hbm, dec),
                (enc_hbm, enc),
                (v_hbm.at[0, 0], vs),
                (g_hbm.at[0, 0], gs),
            )
        )
    ]
    for copy in copies:
        copy.start()
    for copy in copies[:4]:
        copy.wait()
    q = qs[...]
    k = ks[...]
    length = q.shape[0]
    column = jnp.broadcast_to(enc[...].astype(F32), (128, length)).T[:, :1]
    scores = dot(k, q, LAST) * inverse_root
    scores = jnp.where(column == dec[...].astype(F32), scores, -jnp.inf)
    exps = jnp.exp(scores - jnp.max(scores, axis=0, keepdims=True))
    probs = exps / jnp.sum(exps, axis=0, keepdims=True)
    for copy in copies[4:]:
        copy.wait()
    g = gs[...]
    dprobs = dot(vs[...], g, LAST)
    delta = jnp.sum(probs * dprobs, axis=0, keepdims=True)
    dscores = (probs * (dprobs - delta) * inverse_root).astype(BF16)
    both_ref[:, :HD] = dot(dscores, q, PLAIN).astype(BF16)
    both_ref[:, HD:] = dot(probs.astype(BF16), g, PLAIN).astype(BF16)
    gq_ref[0, 0] = dot(dscores, k, FIRST).astype(BF16)


def both_of(a, b):
    return (a[0] ^ b[0], a[1] ^ b[1])


def terms(both_ref, wk_ref, wv_ref, bit, use):
    low, x, _ = place()
    for m in (1, 2, 3, 0):
        for n in range(2):
            block = (jnp.bitwise_xor(low, n) * 4 + jnp.bitwise_xor(x, m)) * 2 + bit
            rows = pl.ds(pl.multiple_of(block * 256, 256), 256)
            value = dot(both_ref[:, :HD], wk_ref[0, rows, :], LAST)
            use(m, n, value + dot(both_ref[:, HD:], wv_ref[0, rows, :], LAST))


def other_core_kernel(both_ref, wk_ref, wv_ref, out_ref, copy_ref):
    _, _, core = place()

    def use(m, n, value):
        out_ref[m, n] = value.astype(BF16)

    copy_ref[...] = both_ref[...]
    terms(both_ref, wk_ref, wv_ref, 1 - core, use)


def own_core_kernel(both_ref, wk_ref, wv_ref, got_ref, *outs):
    _, _, core = place()

    def use(m, n, value):
        total = value + got_ref[m, n].astype(F32)
        at = 0
        for i, count in enumerate(RANGES):
            first, second, third = ORDERS[i]
            kept = [(0, 0), third, second, both_of(second, third)]
            part = total[at : at + count]
            at += count
            if (n, m) in kept:
                outs[2 * i + 1][kept.index((n, m))] = part
            else:
                outs[2 * i][kept.index(both_of((n, m), first))] = part.astype(BF16)

    terms(both_ref, wk_ref, wv_ref, core, use)


def accumulate(total, grads, steps, own, other):
    d = lax.axis_index("dp")
    z = lax.axis_index("seq")
    _, _, core = place()
    for i, step in enumerate(steps):
        u = lax.rem(z + step - 4 * d + 16, 8)
        which = lax.div(u, 4)
        chunk = jnp.where(u < 4, u, lax.rem(u + 2, 4))
        grad = grads[which]
        for refs_of, bit in ((own, core), (other, 1 - core)):
            piece = refs_of[i][...]
            start = chunk * 512 + bit * 256
            if i and steps[i - 1] == step:
                start = start + 128
            rows = pl.ds(pl.multiple_of(start, 128), piece.shape[0])
            total[rows, :] += dot(piece, grad, PLAIN)


def near_kernel(*refs):
    count = len(NEAR)
    own, other = refs[:count], refs[count : 2 * count]
    here_ref, there_ref, total, grads = refs[2 * count :]
    grads[0] = here_ref[...]
    grads[1] = there_ref[...]
    total[...] = jnp.zeros_like(total)
    accumulate(total, grads, NEAR, own, other)


def far_kernel(*refs):
    count = len(FAR)
    own, other = refs[:count], refs[count : 2 * count]
    here_ref, there_ref, _, total, square_ref, grads = refs[2 * count :]
    grads[0] = here_ref[...]
    grads[1] = there_ref[...]
    accumulate(total, grads, FAR, own, other)
    square_ref[...] = jnp.zeros_like(square_ref)
    for i in range(2):
        value = total[:, i * HD : (i + 1) * HD]
        square = jnp.sum(value * value, axis=0, keepdims=True)
        square_ref[0:1, i * 128 : (i + 1) * 128] = square[:, :128] + square[:, 128:]


def encode(row):
    high = row.astype(BF16).astype(F32)
    middle = (row - high).astype(BF16).astype(F32)
    low = row - high - middle
    line = lax.broadcasted_iota(jnp.int32, (16, 256), 0)
    tile = jnp.where(line == 1, middle, jnp.where(line == 2, low, 0.0))
    return jnp.where(line == 0, high, tile).astype(BF16)


def decode(tile):
    return jnp.sum(tile.astype(F32), axis=0, keepdims=True)


def pack_kernel(*refs):
    first_ref, second_ref, came_ref, here_ref, there_ref = refs[:5]
    up_ref, down_ref, keep_ref, square_ref, whole = refs[5:]
    z = lax.axis_index("seq")
    whole[:256, :] = first_ref[0] + came_ref[:256, :].astype(F32)
    whole[256:, :] = second_ref[0] + came_ref[256:, :].astype(F32)
    for ref, places in ((up_ref, (2, 3, 4)), (down_ref, (-3, -2)), (keep_ref, (-1, 0, 1))):
        for i, by in enumerate(places):
            start = pl.multiple_of(lax.rem(z + by + 8, 8) * 64, 64)
            ref[i * 64 : (i + 1) * 64, :] = whole[pl.ds(start, 64), :].astype(ref.dtype)
    square_ref[...] = here_ref[...] + there_ref[...]
    tile = encode(square_ref[0:1, :])
    up_ref[192:, :] = tile
    down_ref[128:, :] = tile


def middle_kernel(
    keep_ref, square_ref, up_ref, down_ref, last_ref, next_ref, keep_out, square_out
):
    up = up_ref[:192, :].astype(F32)
    down = down_ref[:128, :].astype(F32)
    keep = keep_ref[...]
    last_ref[:64, :] = (keep[:64] + up[:64]).astype(BF16)
    next_ref[:64, :] = (keep[128:] + up[128:] + down[64:]).astype(BF16)
    keep_out[...] = keep[64:128] + up[64:128] + down[:64]
    behind = square_ref[0:1, :] + decode(up_ref[192:, :])
    around = behind + decode(down_ref[128:, :])
    square_out[...] = jnp.broadcast_to(around, square_out.shape)
    last_ref[64:, :] = encode(behind)
    next_ref[64:, :] = encode(around)


def finish_kernel(
    keep_ref,
    around_ref,
    last_ref,
    next_ref,
    total,
    enc_ref,
    key_ref,
    value_ref,
    scaled,
    enc,
    sems,
):
    enc[...] = keep_ref[...] + last_ref[:64, :].astype(F32) + next_ref[:64, :].astype(F32)
    copies = [pltpu.make_async_copy(enc, enc_ref.at[0], sems.at[2, 0])]
    copies[0].start()
    squares = around_ref[0:1, :] + decode(last_ref[64:, :]) + decode(next_ref[64:, :])
    for i, ref in enumerate((key_ref, value_ref)):
        square = jnp.sum(squares[:, i * 128 : (i + 1) * 128], axis=1, keepdims=True)
        factor = 1.0 / jnp.sqrt(square / (D * H * HD) + 1e-06)
        for j in range(4):
            rows = slice(j * 512, (j + 1) * 512)
            scaled[i, rows, :] = total[rows, i * HD : (i + 1) * HD] * factor
            copy = pltpu.make_async_copy(
                scaled.at[i, rows, :], ref.at[0, rows, :], sems.at[i, j]
            )
            copy.start()
            copies.append(copy)
    for copy in copies:
        copy.wait()


def shards(
    enc_out, w_key, w_value, query, key_cache, value_cache, grad_attn, dec_segments, enc_segments
):
    length = query.shape[2]
    columns = query.shape[3]
    shape = jax.ShapeDtypeStruct

    def shift(value, by):
        return lax.ppermute(value, "seq", [(i, (i + by) % 8) for i in range(8)])

    def swap(value, low, x, core):
        mask = low * 8 + x * 2 + core
        return lax.ppermute(value, "pipe", [(i, i ^ mask) for i in range(16)])

    (piece,) = call(
        half_kernel,
        (shape((256, length), BF16),),
        (enc_out,),
        (HB,),
        scratch=(VM((length, 256), BF16), DMA),
        limit=FULL,
        size=MIB,
    )
    pairs = []
    for b in range(2):
        for z in range(8):
            to = (z + 2) % 8 if z in (2, 3, 6, 7) else (z - 2) % 8
            inside = z // 4 == b
            pairs.append((b * 8 + z, b * 8 + z if inside else (1 - b) * 8 + to))
    held = lax.ppermute(piece, ("dp", "seq"), pairs)

    line = VM((length, columns), BF16)
    grad_query, both = call(
        attention_kernel,
        (shape((1, 1, length, columns), BF16), shape((length, 2 * columns), BF16)),
        (dec_segments, enc_segments, query, key_cache, value_cache, grad_attn),
        (HB,) * 6,
        scratch=(VM((1, length), jnp.int32),) * 2 + (line,) * 4 + (DMA((6,)),),
        limit=ATTN,
        flops=5 * 2 * 512 * 512 * 256,
        size=2 * MIB,
    )
    sent, both = call(
        other_core_kernel,
        (shape((4, 2, length, 256), BF16), shape((length, 2 * columns), BF16)),
        (both, w_key, w_value),
        (VM,) * 3,
        limit=8,
        flops=1 << 30,
        size=5 * MIB,
    )
    there = lax.ppermute(both, "dp", [(0, 1), (1, 0)])
    got = swap(sent, 0, 0, 1)

    ahead = [held] + [shift(held, k) for k in (1, 2)]
    behind = [held] + [shift(held, -k) for k in (1, 2)]
    ahead.append(shift(ahead[2], 1))
    behind.append(shift(behind[2], -1))
    far = (shift(ahead[2][:128], 2), shift(behind[2][128:], -2))

    out = []
    for count in RANGES:
        out += [shape((4, count, 256), BF16), shape((4, count, 256), F32)]
    out = call(
        own_core_kernel,
        tuple(out),
        (both, w_key, w_value, got),
        (VM,) * 4,
        limit=8,
        flops=1 << 30,
        size=8 * MIB,
    )
    kept = [out[2 * i + 1] for i in range(2)]
    sent = [out[2 * i] for i in range(2)]
    for stage in range(2):
        came = [
            swap(sent[i], ORDERS[i][stage][0], ORDERS[i][stage][1], 0)
            for i in range(2)
        ]
        total = [kept[i] + came[i].astype(F32) for i in range(2)]
        half = 2 - stage
        kept = [value[:half] for value in total]
        sent = [value[half:].astype(BF16) for value in total]
    came = swap(jnp.concatenate(sent, axis=1)[0], 1, 0, 0)

    own = [held, ahead[1], behind[1], ahead[2], behind[2]]
    other = [swap(value, 0, 0, 1) for value in own]
    grads = VM((2, length, 2 * HD), BF16)
    sums = shape((2048, 2 * HD), F32)
    (total,) = call(
        near_kernel,
        (sums,),
        (*own, *other, both, there),
        (VM,) * 12,
        scratch=(grads,),
        limit=8,
        flops=5 << 28,
        size=8 * MIB,
    )
    own = [ahead[3], behind[3], *far]
    other = [swap(value, 0, 0, 1) for value in own]
    total, square = call(
        far_kernel,
        (sums, shape((8, 256), F32)),
        (*own, *other, both, there, total),
        (VM,) * 11,
        scratch=(grads,),
        limit=8,
        flops=3 << 28,
        size=8 * MIB,
        alias={10: 0},
    )
    square_there = lax.ppermute(square, "dp", [(0, 1), (1, 0)])
    up, down, keep, square = call(
        pack_kernel,
        (
            shape((208, 256), BF16),
            shape((144, 256), BF16),
            shape((192, 256), F32),
            shape((8, 256), F32),
        ),
        (*kept, came, square, square_there),
        (VM,) * 5,
        scratch=(VM((length, 256), F32),),
        limit=4,
        size=2 * MIB,
    )
    up = shift(up, 3)
    down = shift(down, -3)
    last, following, keep, square = call(
        middle_kernel,
        (
            shape((80, 256), BF16),
            shape((80, 256), BF16),
            shape((64, 256), F32),
            shape((8, 256), F32),
        ),
        (keep, square, up, down),
        (VM,) * 4,
        limit=4,
        size=MIB,
    )
    last = shift(last, -1)
    following = shift(following, 1)
    grad_enc, grad_wkey, grad_wvalue = call(
        finish_kernel,
        (shape((1, 64, 256), F32), *(shape((1, 2048, HD), F32),) * 2),
        (keep, square, last, following, total),
        (VM,) * 5,
        outs=(HB, HB, HB),
        scratch=(VM((2, 2048, HD), F32), VM((64, 256), F32), DMA((3, 4))),
        limit=12,
        size=8 * MIB,
    )
    return (grad_query, grad_enc, grad_wkey, grad_wvalue)


def solution(mesh):
    in_specs = (
        P("dp", None, "seq"),
        P("pipe", None, "seq"),
        P("pipe", None, "seq"),
        P("pipe", "dp", None, "seq"),
        P("pipe", "dp", None, "seq"),
        P("pipe", "dp", None, "seq"),
        P("pipe", "dp", None, "seq"),
        P("dp", None),
        P("dp", None),
    )
    out_specs = (
        P("pipe", "dp", None, "seq"),
        P("dp", "seq", "pipe"),
        P("pipe", "dp", "seq"),
        P("pipe", "dp", "seq"),
    )
    return jax.shard_map(
        shards, mesh=mesh, in_specs=in_specs, out_specs=out_specs, check_vma=False
    )
```

```python
import math

import jax
import jax.numpy as jnp
from jax import lax
from jax.experimental import pallas as pl
from jax.experimental.pallas import tpu as pltpu
from jax.sharding import PartitionSpec as P


D = 4096
H = 8
HD = 256


F32 = jnp.float32
BF16 = jnp.bfloat16
LAST = (((1,), (1,)), ((), ()))
FIRST = (((0,), (0,)), ((), ()))
PLAIN = (((1,), (0,)), ((), ()))
VM = pltpu.VMEM
HB = pltpu.HBM
DMA = pltpu.SemaphoreType.DMA
MIB = 1 << 20
FULL = 63
ATTN = 54
X1, X3, Y1 = (0, 1), (0, 3), (1, 0)
ORDERS = ((X1, X3, Y1), (X3, X1, Y1))
RANGES = (256, 256)
NEAR = (0, -1, 1, -2, 2)
FAR = (-3, 3, 4, 4)


def dot(a, b, dims):
    return lax.dot_general(a, b, dims, preferred_element_type=F32)


def call(kernel, out, ins, spaces, outs=None, scratch=(), limit=12, flops=0, size=0, alias=None):
    outs = outs or (VM,) * len(out)
    return pl.pallas_call(
        kernel,
        out_shape=out,
        in_specs=[pl.BlockSpec(memory_space=m) for m in spaces],
        out_specs=tuple(pl.BlockSpec(memory_space=m) for m in outs),
        scratch_shapes=list(scratch),
        input_output_aliases=alias or {},
        compiler_params=pltpu.CompilerParams(vmem_limit_bytes=limit * MIB),
        cost_estimate=pl.CostEstimate(flops=flops, bytes_accessed=size, transcendentals=0),
    )(*ins)


def place():
    at = lax.axis_index("pipe")
    core = lax.rem(at, 2)
    x = lax.rem(lax.div(at, 2), 4)
    low = lax.div(at, 8)
    return low, x, core


def half_kernel(enc_ref, out_ref, block, sem):
    _, _, core = place()
    start = pl.multiple_of(core * 256, 256)
    copy = pltpu.make_async_copy(enc_ref.at[0, :, pl.ds(start, 256)], block, sem)
    copy.start()
    copy.wait()
    out_ref[...] = block[...].astype(F32).T.astype(BF16)


def attention_kernel(
    dec_hbm, enc_hbm, q_hbm, k_hbm, v_hbm, g_hbm, gq_ref, both_ref, dec, enc, qs, ks, vs, gs, sems
):
    inverse_root = 1.0 / math.sqrt(HD)
    copies = [
        pltpu.make_async_copy(src, dst, sems.at[i])
        for i, (src, dst) in enumerate(
            (
                (k_hbm.at[0, 0], ks),
                (q_hbm.at[0, 0], qs),
                (dec_hbm, dec),
                (enc_hbm, enc),
                (v_hbm.at[0, 0], vs),
                (g_hbm.at[0, 0], gs),
            )
        )
    ]
    for copy in copies:
        copy.start()
    for copy in copies[:4]:
        copy.wait()
    q = qs[...]
    k = ks[...]
    length = q.shape[0]
    column = jnp.broadcast_to(enc[...].astype(F32), (128, length)).T[:, :1]
    scores = dot(k, q, LAST) * inverse_root
    scores = jnp.where(column == dec[...].astype(F32), scores, -jnp.inf)
    exps = jnp.exp(scores - jnp.max(scores, axis=0, keepdims=True))
    probs = exps / jnp.sum(exps, axis=0, keepdims=True)
    for copy in copies[4:]:
        copy.wait()
    g = gs[...]
    dprobs = dot(vs[...], g, LAST)
    delta = jnp.sum(probs * dprobs, axis=0, keepdims=True)
    dscores = (probs * (dprobs - delta) * inverse_root).astype(BF16)
    both_ref[:, :HD] = dot(dscores, q, PLAIN).astype(BF16)
    both_ref[:, HD:] = dot(probs.astype(BF16), g, PLAIN).astype(BF16)
    gq_ref[0, 0] = dot(dscores, k, FIRST).astype(BF16)


def both_of(a, b):
    return (a[0] ^ b[0], a[1] ^ b[1])


def terms(both_ref, wk_ref, wv_ref, bit, use):
    low, x, _ = place()
    for m in (1, 2, 3, 0):
        for n in range(2):
            block = (jnp.bitwise_xor(low, n) * 4 + jnp.bitwise_xor(x, m)) * 2 + bit
            rows = pl.ds(pl.multiple_of(block * 256, 256), 256)
            value = dot(both_ref[:, :HD], wk_ref[0, rows, :], LAST)
            use(m, n, value + dot(both_ref[:, HD:], wv_ref[0, rows, :], LAST))


def other_core_kernel(both_ref, wk_ref, wv_ref, out_ref, copy_ref):
    _, _, core = place()

    def use(m, n, value):
        out_ref[m, n] = value.astype(BF16)

    copy_ref[...] = both_ref[...]
    terms(both_ref, wk_ref, wv_ref, 1 - core, use)


def own_core_kernel(both_ref, wk_ref, wv_ref, got_ref, *outs):
    _, _, core = place()

    def use(m, n, value):
        total = value + got_ref[m, n].astype(F32)
        at = 0
        for i, count in enumerate(RANGES):
            first, second, third = ORDERS[i]
            kept = [(0, 0), third, second, both_of(second, third)]
            part = total[at : at + count]
            at += count
            if (n, m) in kept:
                outs[2 * i + 1][kept.index((n, m))] = part
            else:
                outs[2 * i][kept.index(both_of((n, m), first))] = part.astype(BF16)

    terms(both_ref, wk_ref, wv_ref, core, use)


def accumulate(total, grads, steps, own, other):
    d = lax.axis_index("dp")
    z = lax.axis_index("seq")
    _, _, core = place()
    for i, step in enumerate(steps):
        u = lax.rem(z + step - 4 * d + 16, 8)
        which = lax.div(u, 4)
        chunk = jnp.where(u < 4, u, lax.rem(u + 2, 4))
        grad = grads[which]
        for refs_of, bit in ((own, core), (other, 1 - core)):
            piece = refs_of[i][...]
            start = chunk * 512 + bit * 256
            if i and steps[i - 1] == step:
                start = start + 128
            rows = pl.ds(pl.multiple_of(start, 128), piece.shape[0])
            total[rows, :] += dot(piece, grad, PLAIN)


def near_kernel(*refs):
    count = len(NEAR)
    own, other = refs[:count], refs[count : 2 * count]
    here_ref, there_ref, total, grads = refs[2 * count :]
    grads[0] = here_ref[...]
    grads[1] = there_ref[...]
    total[...] = jnp.zeros_like(total)
    accumulate(total, grads, NEAR, own, other)


def far_kernel(*refs):
    count = len(FAR)
    own, other = refs[:count], refs[count : 2 * count]
    here_ref, there_ref, _, total, square_ref, grads = refs[2 * count :]
    grads[0] = here_ref[...]
    grads[1] = there_ref[...]
    accumulate(total, grads, FAR, own, other)
    square_ref[...] = jnp.zeros_like(square_ref)
    for i in range(2):
        value = total[:, i * HD : (i + 1) * HD]
        square = jnp.sum(value * value, axis=0, keepdims=True)
        square_ref[0:1, i * 128 : (i + 1) * 128] = square[:, :128] + square[:, 128:]


def encode(row):
    high = row.astype(BF16).astype(F32)
    middle = (row - high).astype(BF16).astype(F32)
    low = row - high - middle
    line = lax.broadcasted_iota(jnp.int32, (16, 256), 0)
    tile = jnp.where(line == 1, middle, jnp.where(line == 2, low, 0.0))
    return jnp.where(line == 0, high, tile).astype(BF16)


def decode(tile):
    return jnp.sum(tile.astype(F32), axis=0, keepdims=True)


def pack_kernel(first_ref, second_ref, came_ref, up_ref, down_ref, keep_ref, whole):
    z = lax.axis_index("seq")
    whole[:256, :] = first_ref[0] + came_ref[:256, :].astype(F32)
    whole[256:, :] = second_ref[0] + came_ref[256:, :].astype(F32)
    for ref, places in ((up_ref, (1, -2)), (down_ref, (-1, -4, 2)), (keep_ref, (0, -3, 3))):
        for i, by in enumerate(places):
            start = pl.multiple_of(lax.rem(z + by + 8, 8) * 64, 64)
            ref[i * 64 : (i + 1) * 64, :] = whole[pl.ds(start, 64), :].astype(ref.dtype)


def middle_kernel(
    keep_ref,
    up_ref,
    down_ref,
    square_ref,
    behind_ref,
    after_ref,
    last_ref,
    next_ref,
    keep_out,
    square_out,
):
    up = up_ref[...].astype(F32)
    down = down_ref[...].astype(F32)
    keep = keep_ref[...]
    keep_out[...] = keep[:64] + up[:64] + down[:64]
    last_ref[:64, :] = (keep[64:128] + up[64:] + down[64:128]).astype(BF16)
    next_ref[:64, :] = (keep[128:] + down[128:]).astype(BF16)
    after = square_ref[0:1, :] + after_ref[0:1, :]
    around = after + behind_ref[0:1, :]
    square_out[...] = jnp.broadcast_to(around, square_out.shape)
    last_ref[64:, :] = encode(around)
    next_ref[64:, :] = encode(after)


def finish_kernel(
    keep_ref,
    around_ref,
    last_ref,
    next_ref,
    total,
    enc_ref,
    key_ref,
    value_ref,
    scaled,
    enc,
    sems,
):
    enc[...] = keep_ref[...] + last_ref[:64, :].astype(F32) + next_ref[:64, :].astype(F32)
    copies = [pltpu.make_async_copy(enc, enc_ref.at[0], sems.at[2, 0])]
    copies[0].start()
    squares = around_ref[0:1, :] + decode(last_ref[64:, :]) + decode(next_ref[64:, :])
    for i, ref in enumerate((key_ref, value_ref)):
        square = jnp.sum(squares[:, i * 128 : (i + 1) * 128], axis=1, keepdims=True)
        factor = 1.0 / jnp.sqrt(square / (D * H * HD) + 1e-06)
        for j in range(4):
            rows = slice(j * 512, (j + 1) * 512)
            scaled[i, rows, :] = total[rows, i * HD : (i + 1) * HD] * factor
            copy = pltpu.make_async_copy(
                scaled.at[i, rows, :], ref.at[0, rows, :], sems.at[i, j]
            )
            copy.start()
            copies.append(copy)
    for copy in copies:
        copy.wait()


def shards(
    enc_out, w_key, w_value, query, key_cache, value_cache, grad_attn, dec_segments, enc_segments
):
    length = query.shape[2]
    columns = query.shape[3]
    shape = jax.ShapeDtypeStruct

    def shift(value, by):
        return lax.ppermute(value, "seq", [(i, (i + by) % 8) for i in range(8)])

    def swap(value, low, x, core):
        mask = low * 8 + x * 2 + core
        return lax.ppermute(value, "pipe", [(i, i ^ mask) for i in range(16)])

    (piece,) = call(
        half_kernel,
        (shape((256, length), BF16),),
        (enc_out,),
        (HB,),
        scratch=(VM((length, 256), BF16), DMA),
        limit=FULL,
        size=MIB,
    )
    pairs = []
    for b in range(2):
        for z in range(8):
            to = (z + 2) % 8 if z in (2, 3, 6, 7) else (z - 2) % 8
            inside = z // 4 == b
            pairs.append((b * 8 + z, b * 8 + z if inside else (1 - b) * 8 + to))
    held = lax.ppermute(piece, ("dp", "seq"), pairs)

    line = VM((length, columns), BF16)
    grad_query, both = call(
        attention_kernel,
        (shape((1, 1, length, columns), BF16), shape((length, 2 * columns), BF16)),
        (dec_segments, enc_segments, query, key_cache, value_cache, grad_attn),
        (HB,) * 6,
        scratch=(VM((1, length), jnp.int32),) * 2 + (line,) * 4 + (DMA((6,)),),
        limit=ATTN,
        flops=5 * 2 * 512 * 512 * 256,
        size=2 * MIB,
    )
    sent, both = call(
        other_core_kernel,
        (shape((4, 2, length, 256), BF16), shape((length, 2 * columns), BF16)),
        (both, w_key, w_value),
        (VM,) * 3,
        limit=8,
        flops=1 << 30,
        size=5 * MIB,
    )
    there = lax.ppermute(both, "dp", [(0, 1), (1, 0)])
    got = swap(sent, 0, 0, 1)

    ahead = [held] + [shift(held, k) for k in (1, 2)]
    behind = [held] + [shift(held, -k) for k in (1, 2)]
    ahead.append(shift(ahead[2], 1))
    behind.append(shift(behind[2], -1))
    far = (shift(ahead[2][:128], 2), shift(behind[2][128:], -2))

    out = []
    for count in RANGES:
        out += [shape((4, count, 256), BF16), shape((4, count, 256), F32)]
    out = call(
        own_core_kernel,
        tuple(out),
        (both, w_key, w_value, got),
        (VM,) * 4,
        limit=8,
        flops=1 << 30,
        size=8 * MIB,
    )
    kept = [out[2 * i + 1] for i in range(2)]
    sent = [out[2 * i] for i in range(2)]
    for stage in range(2):
        came = [
            swap(sent[i], ORDERS[i][stage][0], ORDERS[i][stage][1], 0)
            for i in range(2)
        ]
        total = [kept[i] + came[i].astype(F32) for i in range(2)]
        half = 2 - stage
        kept = [value[:half] for value in total]
        sent = [value[half:].astype(BF16) for value in total]
    came = swap(jnp.concatenate(sent, axis=1)[0], 1, 0, 0)

    own = [held, ahead[1], behind[1], ahead[2], behind[2]]
    other = [swap(value, 0, 0, 1) for value in own]
    grads = VM((2, length, 2 * HD), BF16)
    sums = shape((2048, 2 * HD), F32)
    (total,) = call(
        near_kernel,
        (sums,),
        (*own, *other, both, there),
        (VM,) * 12,
        scratch=(grads,),
        limit=8,
        flops=5 << 28,
        size=8 * MIB,
    )
    own = [ahead[3], behind[3], *far]
    other = [swap(value, 0, 0, 1) for value in own]
    total, square = call(
        far_kernel,
        (sums, shape((8, 256), F32)),
        (*own, *other, both, there, total),
        (VM,) * 11,
        scratch=(grads,),
        limit=8,
        flops=3 << 28,
        size=8 * MIB,
        alias={10: 0},
    )
    square_there = lax.ppermute(square, "dp", [(0, 1), (1, 0)])
    up, down, keep = call(
        pack_kernel,
        (shape((128, 256), BF16), shape((192, 256), BF16), shape((192, 256), F32)),
        (*kept, came),
        (VM,) * 3,
        scratch=(VM((length, 256), F32),),
        limit=4,
        size=2 * MIB,
    )
    up = shift(up, 1)
    down = shift(down, -1)
    square = square + square_there
    behind = shift(square, 1)
    after = shift(square, -1)
    last, following, keep, square = call(
        middle_kernel,
        (
            shape((80, 256), BF16),
            shape((80, 256), BF16),
            shape((64, 256), F32),
            shape((8, 256), F32),
        ),
        (keep, up, down, square, behind, after),
        (VM,) * 6,
        limit=4,
        size=MIB,
    )
    last = shift(last, -3)
    following = shift(following, 3)
    grad_enc, grad_wkey, grad_wvalue = call(
        finish_kernel,
        (shape((1, 64, 256), F32), *(shape((1, 2048, HD), F32),) * 2),
        (keep, square, last, following, total),
        (VM,) * 5,
        outs=(HB, HB, HB),
        scratch=(VM((2, 2048, HD), F32), VM((64, 256), F32), DMA((3, 4))),
        limit=12,
        size=8 * MIB,
    )
    return (grad_query, grad_enc, grad_wkey, grad_wvalue)


def solution(mesh):
    in_specs = (
        P("dp", None, "seq"),
        P("pipe", None, "seq"),
        P("pipe", None, "seq"),
        P("pipe", "dp", None, "seq"),
        P("pipe", "dp", None, "seq"),
        P("pipe", "dp", None, "seq"),
        P("pipe", "dp", None, "seq"),
        P("dp", None),
        P("dp", None),
    )
    out_specs = (
        P("pipe", "dp", None, "seq"),
        P("dp", "seq", "pipe"),
        P("pipe", "dp", "seq"),
        P("pipe", "dp", "seq"),
    )
    return jax.shard_map(
        shards, mesh=mesh, in_specs=in_specs, out_specs=out_specs, check_vma=False
    )
```
